32 devices in a mesh: dp: 32 (over z, y, x, core).
Axes of the slice: x: 2, y: 2, z: 4, core: 2. Of those that a mesh axis runs over, the one named last changes fastest.
Arguments:
- layer_input: bfloat16 [32, 1024, 768], P('dp'), may hold values from -6 to 6
- segments: int32 [32, 1024], P('dp'), may hold values from 0 to 15, never falling along the last dimension, each value on 1 to 512 neighbouring positions
- cotangent: bfloat16 [32, 1024, 768], P('dp'), may hold values from -6 to 6
- w_query: bfloat16 [768, 768], P('dp'), may hold values from -0.21875 to 0.21875
- b_query: bfloat16 [768], P('dp'), may hold values from -1.1953125 to 1.1953125
- w_key: bfloat16 [768, 768], P('dp'), may hold values from -0.21875 to 0.21875
- w_value: bfloat16 [768, 768], P('dp'), may hold values from -0.21875 to 0.21875
- b_value: bfloat16 [768], P('dp'), may hold values from -1.1953125 to 1.1953125
- w_out: bfloat16 [768, 768], P('dp'), may hold values from -1.75 to 1.75
- b_out: bfloat16 [768], P('dp'), may hold values from -1.1953125 to 1.1953125
- norm1_gain: bfloat16 [768], P('dp'), may hold values from 0.5 to 1.5
- norm1_bias: bfloat16 [768], P('dp'), may hold values from -1.1953125 to 1.1953125
- w_in: bfloat16 [768, 3072], P('dp'), may hold values from -0.21875 to 0.21875
- b_in: bfloat16 [3072], P('dp'), may hold values from -1.1953125 to 1.1953125
- w_down: bfloat16 [3072, 768], P('dp'), may hold values from -0.109375 to 0.109375
- b_down: bfloat16 [768], P('dp'), may hold values from -1.1953125 to 1.1953125
- norm2_gain: bfloat16 [768], P('dp'), may hold values from 0.5 to 1.5
- norm2_bias: bfloat16 [768], P('dp'), may hold values from -1.1953125 to 1.1953125
Outputs:
- layer_out: bfloat16 [32, 1024, 768], P('dp')
- grad_input: float32 [32, 1024, 768], P('dp')
- grad_w_query: float32 [768, 768], P('dp')
- grad_b_query: float32 [768], P('dp')
- grad_w_key: float32 [768, 768], P('dp')
- grad_w_value: float32 [768, 768], P('dp')
- grad_b_value: float32 [768], P('dp')
- grad_w_out: float32 [768, 768], P('dp')
- grad_b_out: float32 [768], P('dp')
- grad_norm1_gain: float32 [768], P('dp')
- grad_norm1_bias: float32 [768], P('dp')
- grad_w_in: float32 [768, 3072], P('dp')
- grad_b_in: float32 [3072], P('dp')
- grad_w_down: float32 [3072, 768], P('dp')
- grad_b_down: float32 [768], P('dp')
- grad_norm2_gain: float32 [768], P('dp')
- grad_norm2_bias: float32 [768], P('dp')
The draws below stay inside these ranges and needn't reach their ends.
Inputs may be any that keep to these rules, and one draw needn't show every extreme that they name: `segments`: segment numbers never fall along a sequence; a document has at most 512 tokens, and some document has exactly that many.
All inputs are finite; a program needn't handle non-finite values.
Results may differ from the reference program's by a relative error of at most 0.014.
Values may be sent and summed in bfloat16 or wider, within the bound.
No kernel may reach another device: no remote copies, remote signals or barrier semaphores. Data moves between devices by JAX's collectives and lax.ppermute only.
A program may use at most 256 MiB of HBM per device.

```python
import math
import jax
import jax.numpy as jnp
import numpy as np
from jax import lax

D = 768
HEADS = 12
HEAD_DIM = 64
FF = 3072
SEQ_LEN = 1024
SEQS = 32
DOCS = 16
LONGEST = 512


def with_spikes(entries, own_key, source, target, blocks, factor):
    def block_of(dim):
        return (jnp.arange(entries.shape[dim]) // (entries.shape[dim] // blocks)).reshape((-1,) + (1,) * (entries.ndim - 1 - dim))

    one_side = jax.random.permutation(own_key, blocks)[block_of(target)]
    other_side = (block_of(target) + blocks // 2) % blocks
    return jnp.where((block_of(source) == one_side) | (block_of(source) == other_side), factor * entries, entries)


def block_levels(own_key, dims, pieces, least, top_value):
    factor_of = 1.0
    for dim, blocks in pieces:
        steps = jax.random.uniform(jax.random.fold_in(jax.random.fold_in(own_key, 6), dim), (blocks,), jnp.float32, least / len(pieces), top_value / len(pieces))
        factor_of = factor_of * jnp.repeat(jnp.exp(steps), dims[dim] // blocks).reshape((-1,) + (1,) * (len(dims) - 1 - dim))
    return factor_of


def split_up(number_of, total, bound, slope):
    weights = [(1 << 20) // math.isqrt(rank ** slope) + 1 for rank in range(2, number_of + 1)]
    spare, given = total - bound - (number_of - 1), [1] * (number_of - 1)
    while spare > 0:
        free = [i for i in range(number_of - 1) if given[i] < bound]
        mass, left = sum([weights[i] for i in free]), spare
        for i in free:
            addition = min(bound - given[i], max(1, left * weights[i] // mass), spare)
            given[i] = given[i] + addition
            spare = spare - addition
    return np.array([bound] + given)


def uneven_parts(own_key, count, total, reach, lean):
    if count == 2:
        one = jax.random.randint(own_key, (), max(1, total - reach), min(reach, total - 1) + 1)
        return jnp.stack([one, total - one])
    lengths = jnp.asarray(split_up(count, total, reach, lean), jnp.int32)
    twos = (count - 1) // 2
    giver, receiver = lengths[1:1 + 2 * twos:2], lengths[2:2 + 2 * twos:2]
    room = jnp.minimum(giver - 1, reach - receiver)
    moved = jax.random.randint(jax.random.fold_in(own_key, 1), (twos,), 0, 1 << 20) % (room + 1)
    lengths = lengths.at[1:1 + 2 * twos:2].set(giver - moved).at[2:2 + 2 * twos:2].set(receiver + moved)
    return lengths[jax.random.permutation(jax.random.fold_in(own_key, 2), count)]


def gaussian(key, dims, spread, most, cuts=(), kind=jnp.bfloat16):
    loudness = block_levels(key, dims, cuts, -0.22, 0.18) if cuts else 1.0
    array = jax.random.normal(key, dims, jnp.float32) * spread * loudness
    return jnp.minimum(jnp.maximum(array, -most), most).astype(kind)


def gaussian_with(own_key, shape, deviation, most, pieces, heavy, kind=jnp.bfloat16):
    drawn = deviation * jax.random.normal(own_key, shape, jnp.float32)
    if pieces:
        drawn = drawn * block_levels(own_key, shape, pieces, -0.22, 0.18)
    return jnp.clip(with_spikes(drawn, jax.random.fold_in(own_key, 3), *heavy), -most, most).astype(kind)


def setup_inputs(seed: int = 0) -> dict:
    key_list = jax.random.split(jax.random.key(seed), 19)
    return {
        "layer_input": gaussian(key_list[0], (SEQS, SEQ_LEN, D), 1.0, 6.0, ((0, 32),)),
        "segments": jax.vmap(lambda own: jnp.searchsorted(jnp.cumsum(uneven_parts(own, DOCS, SEQ_LEN, LONGEST, 2)), jnp.arange(SEQ_LEN), side="right"))(jax.random.split(key_list[1], SEQS)).reshape((SEQS, SEQ_LEN)).astype(jnp.int32),
        "cotangent": gaussian_with(key_list[2], (SEQS, SEQ_LEN, D), 1.0, 6.0, ((0, 32),), (0, 2, 32, 2.75)),
        "w_query": gaussian(key_list[3], (D, D), D ** -0.5, 0.21875, ((0, 32),)),
        "b_query": gaussian(key_list[4], (D,), 0.3, 1.1953125, ((0, 32),)),
        "w_key": gaussian(key_list[5], (D, D), D ** -0.5, 0.21875, ((0, 32),)),
        "w_value": gaussian(key_list[6], (D, D), D ** -0.5, 0.21875, ((0, 32),)),
        "b_value": gaussian(key_list[7], (D,), 0.3, 1.1953125, ((0, 32),)),
        "w_out": gaussian(key_list[8], (D, D), (D // 64) ** -0.5, 1.75, ((0, 32),)),
        "b_out": gaussian(key_list[9], (D,), 0.3, 1.1953125, ((0, 32),)),
        "norm1_gain": jnp.clip(1.0 + 0.1 * jax.random.normal(key_list[10], (D,), jnp.float32), 0.5, 1.5).astype(jnp.bfloat16),
        "norm1_bias": gaussian(key_list[11], (D,), 0.3, 1.1953125, ((0, 32),)),
        "w_in": gaussian(key_list[12], (D, FF), D ** -0.5, 0.21875, ((0, 32),)),
        "b_in": gaussian(key_list[13], (FF,), 0.3, 1.1953125, ((0, 32),)),
        "w_down": gaussian(key_list[14], (FF, D), FF ** -0.5, 0.109375, ((0, 32),)),
        "b_down": gaussian(key_list[15], (D,), 0.3, 1.1953125, ((0, 32),)),
        "norm2_gain": jnp.clip(1.0 + 0.1 * jax.random.normal(key_list[16], (D,), jnp.float32), 0.5, 1.5).astype(jnp.bfloat16),
        "norm2_bias": gaussian(key_list[17], (D,), 0.3, 1.1953125, ((0, 32),)),
    }


@jax.custom_vjp
def low(v):
    return lax.optimization_barrier(v.astype(jnp.bfloat16)).astype(jnp.float32)

@jax.custom_vjp
def low_back(v):
    return v

def low_keep(v):
    return (low(v), None)

def low_pass(kept, grad):
    return (grad,)

def back_keep(v):
    return (v, None)

def back_low(kept, grad):
    return (low(grad),)
low.defvjp(low_keep, low_pass)
low_back.defvjp(back_keep, back_low)

def layer_norm(resid, gain, shift):
    row_mean = lax.optimization_barrier(jnp.mean(resid, axis=-1, keepdims=True))
    centred = resid - row_mean
    variance = lax.optimization_barrier(jnp.mean(centred * centred, axis=-1, keepdims=True))
    return centred * lax.rsqrt(variance + 1e-05) * gain + shift

def product(left, right):
    return jnp.dot(left, right, precision=lax.Precision.HIGHEST)

def attend_one(members):
    q_seq, k_seq, v_seq, doc_ids = members
    raw_scores = jnp.einsum('qhd,khd->hqk', q_seq, k_seq, precision=lax.Precision.HIGHEST) * HEAD_DIM ** (-0.5)
    same_doc = doc_ids[:, None] == doc_ids[None, :]
    scores = low_back(jnp.where(same_doc[None], raw_scores, -1000000000.0))
    attn_prob = low(jax.nn.softmax(scores, axis=-1))
    mixed = jnp.einsum('hqk,khd->qhd', attn_prob, v_seq, precision=lax.Precision.HIGHEST)
    return low(low_back(mixed))

def layer_forward(tok_group, seg_group, params):
    w_query, b_query, w_key, w_value, b_value, w_out, b_out, norm1_gain, norm1_bias, w_in, b_in, w_down, b_down, norm2_gain, norm2_bias = params
    group = tok_group.shape[0]
    tokens_f = low(tok_group).reshape(group * SEQ_LEN, D)
    query = low(low_back(product(tokens_f, low(w_query)) + b_query))
    key_all = low(low_back(product(tokens_f, low(w_key))))
    value = low(low_back(product(tokens_f, low(w_value)) + b_value))
    shape4 = (group, SEQ_LEN, HEADS, HEAD_DIM)
    context = lax.map(jax.checkpoint(attend_one), (query.reshape(shape4), key_all.reshape(shape4), value.reshape(shape4), seg_group))
    context = context.reshape(group * SEQ_LEN, D)
    attn = low_back(product(context, low(w_out)) + b_out)
    hidden1 = layer_norm(tokens_f + attn, norm1_gain, norm1_bias)
    pre_act = low_back(product(low(hidden1), low(w_in)) + b_in)
    activated = low(jax.nn.gelu(pre_act, approximate=False))
    ffn_out = low_back(product(activated, low(w_down)) + b_down)
    result = layer_norm(hidden1 + ffn_out, norm2_gain, norm2_bias)
    return result.reshape(group, SEQ_LEN, D)

def reference(layer_input, segments, cotangent, w_query, b_query, w_key, w_value, b_value, w_out, b_out, norm1_gain, norm1_bias, w_in, b_in, w_down, b_down, norm2_gain, norm2_bias):
    params = tuple((member.astype(jnp.float32) for member in (w_query, b_query, w_key, w_value, b_value, w_out, b_out, norm1_gain, norm1_bias, w_in, b_in, w_down, b_down, norm2_gain, norm2_bias)))
    seq_count = layer_input.shape[0]
    group = 4 if seq_count % 4 == 0 else 1
    input_groups = layer_input.astype(jnp.float32).reshape(seq_count // group, group, SEQ_LEN, D)
    seg_groups = segments.reshape(seq_count // group, group, SEQ_LEN)
    cot_groups = cotangent.astype(jnp.float32).reshape(seq_count // group, group, SEQ_LEN, D)

    def group_step(totals, members):
        tok_group, seg_group, cot_group = members

        def forward(tok_in, param_in):
            return layer_forward(tok_in, seg_group, param_in)
        outputs, pullback = jax.vjp(forward, tok_group, params)
        d_tokens, d_params = pullback(cot_group)
        return (jax.tree.map(jnp.add, totals, d_params), (outputs.astype(jnp.bfloat16), d_tokens))
    zeros = jax.tree.map(jnp.zeros_like, params)
    totals, (outputs, d_tokens) = lax.scan(group_step, zeros, (input_groups, seg_groups, cot_groups))
    return (outputs.reshape(layer_input.shape), d_tokens.reshape(layer_input.shape), totals[0], totals[1], totals[2], totals[3], totals[4], totals[5], totals[6], totals[7], totals[8], totals[9], totals[10], totals[11], totals[12], totals[13], totals[14])
```

```python
import jax
import jax.numpy as jnp
from jax import lax
from jax.sharding import PartitionSpec as P

HEADS = 12


def exact_gelu(values):
    return jax.nn.gelu(values, approximate=False)


def layer_norm(resid, gain, shift):
    row_mean = jnp.mean(resid, axis=-1, keepdims=True)
    centred = resid - row_mean
    variance = jnp.mean(centred * centred, axis=-1, keepdims=True)
    inv_std = lax.rsqrt(variance + 1e-05)
    normed = centred * inv_std
    return (normed * gain + shift, normed, inv_std)


def norm_back(grad_in, gain, normed, inv_std):
    grad_norm = grad_in * gain
    first = jnp.mean(grad_norm, axis=-1, keepdims=True)
    second = jnp.mean(grad_norm * normed, axis=-1, keepdims=True)
    return inv_std * (grad_norm - first - normed * second)


def project(left, weight, bias):
    return jnp.dot(left, weight, preferred_element_type=jnp.float32) + bias.astype(jnp.float32)


def weight_grad(left, right):
    return jnp.einsum("ti,to->io", left, right, preferred_element_type=jnp.float32)


def back_input(grad_rows, weight):
    return jnp.einsum("to,io->ti", grad_rows, weight, preferred_element_type=jnp.float32)


def col_sum(values):
    return jnp.sum(values.astype(jnp.float32), axis=0)


def scatter_sum(matrices, vectors):
    devices = lax.axis_size("dp")
    width = matrices[0].shape[1]
    pieces, shapes = [], []
    for matrix in matrices:
        low = matrix.astype(jnp.bfloat16)
        own = low.shape[0] // devices
        blocks = low.reshape(devices, own, low.shape[1])
        parts = low.shape[1] // width
        pieces += [blocks[:, :, i * width : (i + 1) * width] for i in range(parts)]
        shapes.append((own, parts))
    flat = [vector.reshape(devices, -1) for vector in vectors]
    lengths = [vector.shape[1] for vector in flat]
    packed = jnp.concatenate(flat, axis=1)
    packed = jnp.pad(packed, ((0, 0), (0, 8 * width - packed.shape[1])))
    pieces.append(packed.reshape(devices, 8, width).astype(jnp.bfloat16))
    mine = lax.psum_scatter(
        jnp.concatenate(pieces, axis=1), "dp", scatter_dimension=0, tiled=True
    )[0].astype(jnp.float32)
    outs, at = [], 0
    for own, parts in shapes:
        outs.append(
            jnp.concatenate([mine[at + i * own : at + (i + 1) * own] for i in range(parts)], axis=1)
        )
        at += own * parts
    tail, at = mine[at:].reshape(-1), 0
    for length in lengths:
        outs.append(tail[at : at + length])
        at += length
    return tuple(outs)


def shards(
    layer_input,
    segments,
    cotangent,
    w_query,
    b_query,
    w_key,
    w_value,
    b_value,
    w_out,
    b_out,
    norm1_gain,
    norm1_bias,
    w_in,
    b_in,
    w_down,
    b_down,
    norm2_gain,
    norm2_bias,
):
    low_type = jnp.bfloat16
    wide_type = jnp.float32
    own_rows, width = w_query.shape
    vectors = (b_query, b_value, b_out, norm1_gain, norm1_bias, b_down, norm2_gain, norm2_bias)
    columns = jnp.stack(vectors, axis=1)
    columns = jnp.concatenate([columns, b_in.reshape(own_rows, -1)], axis=1)
    columns = jnp.pad(columns, ((0, 0), (0, 128 - columns.shape[1])))
    first = lax.all_gather(
        jnp.concatenate([w_query, w_key, w_value, columns], axis=1), "dp", axis=0, tiled=True
    )
    second = lax.all_gather(jnp.concatenate([w_out, w_in], axis=1), "dp", axis=0, tiled=True)
    full_wdown = lax.all_gather(w_down, "dp", axis=0, tiled=True)
    full_wq, full_wk, full_wv = (first[:, i * width : (i + 1) * width] for i in range(3))
    rows = first[:, 3 * width :].T
    full_bq, full_bv, full_bo, gain_one, shift_one, full_bdown, gain_two, shift_two = (
        rows[i] for i in range(8)
    )
    full_bin = first[:, 3 * width + 8 : 3 * width + 12].reshape(-1)
    full_wo, full_win = second[:, :width], second[:, width:]
    tokens = layer_input[0]
    doc_ids = segments[0]
    length, model_width = tokens.shape
    head_dim = model_width // HEADS
    scale = head_dim ** (-0.5)
    block_rows = min(512, length)
    blocks = length // block_rows
    query = project(tokens, full_wq, full_bq).astype(low_type)
    key_rows = jnp.dot(tokens, full_wk, preferred_element_type=wide_type).astype(low_type)
    value = project(tokens, full_wv, full_bv).astype(low_type)
    key_heads = key_rows.reshape(length, HEADS, head_dim)
    value_heads = value.reshape(length, HEADS, head_dim)
    query_blocks = query.reshape(blocks, block_rows, HEADS, head_dim)
    doc_blocks = doc_ids.reshape(blocks, block_rows)

    def scores_of(query_part, doc_part):
        raw_scores = (
            jnp.einsum("rhd,khd->hrk", query_part, key_heads, preferred_element_type=wide_type)
            * scale
        )
        same_doc = doc_part[:, None] == doc_ids[None, :]
        return jnp.where(same_doc[None], raw_scores, -1000000000.0)

    def forward_block(members):
        query_part, doc_part = members
        scores = scores_of(query_part, doc_part)
        row_max = jnp.max(scores, axis=-1, keepdims=True)
        expo_vals = jnp.exp(scores - row_max)
        row_total = jnp.sum(expo_vals, axis=-1, keepdims=True)
        attn_prob = (expo_vals / row_total).astype(low_type)
        mixed = jnp.einsum("hrk,khd->rhd", attn_prob, value_heads, preferred_element_type=wide_type)
        return (mixed.astype(low_type), row_max[..., 0] + jnp.log(row_total[..., 0]))

    context_blocks, log_total = lax.map(forward_block, (query_blocks, doc_blocks))
    context = context_blocks.reshape(length, model_width)
    resid_one = tokens.astype(wide_type) + project(context, full_wo, full_bo)
    hidden_one, normed_one, inv_one = layer_norm(
        resid_one, gain_one.astype(wide_type), shift_one.astype(wide_type)
    )
    hidden_low = hidden_one.astype(low_type)
    pre_act = project(hidden_low, full_win, full_bin)
    activated, gelu_pull = jax.vjp(exact_gelu, pre_act)
    act_low = activated.astype(low_type)
    resid_two = hidden_one + project(act_low, full_wdown, full_bdown)
    outputs, normed_two, inv_two = layer_norm(
        resid_two, gain_two.astype(wide_type), shift_two.astype(wide_type)
    )
    layer_out = outputs.astype(low_type)[None]
    grad_out = cotangent[0].astype(wide_type)
    grad_gain_two = jnp.sum(grad_out * normed_two, axis=0)
    grad_shift_two = jnp.sum(grad_out, axis=0)
    grad_resid_two = norm_back(grad_out, gain_two.astype(wide_type), normed_two, inv_two)
    grad_ffn = grad_resid_two.astype(low_type)
    grad_bdown = col_sum(grad_ffn)
    grad_wdown = weight_grad(act_low, grad_ffn)
    grad_act = back_input(grad_ffn, full_wdown)
    grad_pre = gelu_pull(grad_act)[0].astype(low_type)
    grad_bin = col_sum(grad_pre)
    grad_win = weight_grad(hidden_low, grad_pre)
    grad_hidden = grad_resid_two + back_input(grad_pre, full_win)
    grad_gain_one = jnp.sum(grad_hidden * normed_one, axis=0)
    grad_shift_one = jnp.sum(grad_hidden, axis=0)
    grad_resid_one = norm_back(grad_hidden, gain_one.astype(wide_type), normed_one, inv_one)
    grad_attn = grad_resid_one.astype(low_type)
    grad_bo = col_sum(grad_attn)
    grad_wo = weight_grad(context, grad_attn)
    own_wo, own_win, own_wdown, own_bo, own_gain_one, own_shift_one, own_bin, own_bdown, own_gain_two, own_shift_two = (
        scatter_sum(
            (grad_wo, grad_win, grad_wdown),
            (
                grad_bo,
                grad_gain_one,
                grad_shift_one,
                grad_bin,
                grad_bdown,
                grad_gain_two,
                grad_shift_two,
            ),
        )
    )
    grad_context = back_input(grad_attn, full_wo).astype(low_type)
    grad_ctx_blocks = grad_context.reshape(blocks, block_rows, HEADS, head_dim)

    def back_block(carry, members):
        key_acc, value_acc = carry
        query_part, doc_part, total_part, grad_part = members
        scores = scores_of(query_part, doc_part)
        attn_prob = jnp.exp(scores - total_part[..., None])
        grad_prob = jnp.einsum(
            "rhd,khd->hrk", grad_part, value_heads, preferred_element_type=wide_type
        )
        row_dot = jnp.sum(attn_prob * grad_prob, axis=-1, keepdims=True)
        grad_scores = (attn_prob * (grad_prob - row_dot)).astype(low_type)
        grad_q_part = (
            jnp.einsum("hrk,khd->rhd", grad_scores, key_heads, preferred_element_type=wide_type)
            * scale
        )
        key_add = (
            jnp.einsum("hrk,rhd->khd", grad_scores, query_part, preferred_element_type=wide_type)
            * scale
        )
        value_add = jnp.einsum(
            "hrk,rhd->khd", attn_prob.astype(low_type), grad_part, preferred_element_type=wide_type
        )
        return ((key_acc + key_add, value_acc + value_add), grad_q_part)

    zero_heads = jnp.zeros((length, HEADS, head_dim), wide_type)
    (grad_key_acc, grad_value_acc), grad_q_blocks = lax.scan(
        back_block, (zero_heads, zero_heads), (query_blocks, doc_blocks, log_total, grad_ctx_blocks)
    )
    grad_query = grad_q_blocks.reshape(length, model_width).astype(low_type)
    grad_key = grad_key_acc.reshape(length, model_width).astype(low_type)
    grad_value = grad_value_acc.reshape(length, model_width).astype(low_type)
    grad_bq = col_sum(grad_query)
    grad_bv = col_sum(grad_value)
    grad_wq = weight_grad(tokens, grad_query)
    grad_wk = weight_grad(tokens, grad_key)
    grad_wv = weight_grad(tokens, grad_value)
    grad_tokens = (
        grad_resid_one
        + back_input(grad_query, full_wq)
        + back_input(grad_key, full_wk)
        + back_input(grad_value, full_wv)
    )
    attn_mine = scatter_sum((grad_wq, grad_wk, grad_wv), (grad_bq, grad_bv))
    own_wq, own_wk, own_wv, own_bq, own_bv = attn_mine
    return (
        layer_out,
        grad_tokens[None],
        own_wq,
        own_bq,
        own_wk,
        own_wv,
        own_bv,
        own_wo,
        own_bo,
        own_gain_one,
        own_shift_one,
        own_win,
        own_bin,
        own_wdown,
        own_bdown,
        own_gain_two,
        own_shift_two,
    )


def solution(mesh):
    placed = (
        P("dp", None, None),
        P("dp", None),
        P("dp", None, None),
        P("dp", None),
        P("dp"),
        P("dp", None),
        P("dp", None),
        P("dp"),
        P("dp", None),
        P("dp"),
        P("dp"),
        P("dp"),
        P("dp", None),
        P("dp"),
        P("dp", None),
        P("dp"),
        P("dp"),
        P("dp"),
    )
    return jax.shard_map(
        shards,
        mesh=mesh,
        in_specs=placed,
        out_specs=(
            P("dp", None, None),
            P("dp", None, None),
            P("dp", None),
            P("dp"),
            P("dp", None),
            P("dp", None),
            P("dp"),
            P("dp", None),
            P("dp"),
            P("dp"),
            P("dp"),
            P("dp", None),
            P("dp"),
            P("dp", None),
            P("dp"),
            P("dp"),
            P("dp"),
        ),
        check_vma=False,
    )
```

```python
import jax
import jax.numpy as jnp
from jax import lax
from jax.experimental import pallas as pl
from jax.experimental.pallas import tpu as pltpu
from jax.sharding import PartitionSpec as P

HEADS = 12
ROWS = 256
KEYS = 256
PAIRS = 3
PLANE = 8

NT = (((1,), (1,)), ((), ()))


def flipped(values):
    return values.astype(jnp.float32).T


def one_head(values, half):
    lane = lax.broadcasted_iota(jnp.int32, values.shape, 1) % (2 * half)
    return jnp.where(lane < half, values, 0), jnp.where(lane >= half, values, 0)


def head_scores(keys, queries, key_docs, row_docs):
    raw = lax.dot_general(keys, queries, NT, preferred_element_type=jnp.float32)
    return jnp.where(key_docs == row_docs, raw, -1000000000.0)


def attend_kernel(lo_ref, hi_ref, q_ref, k_ref, v_ref, seg_col_ref, seg_row_ref, out_ref, log_ref, km_ref, vt_ref):
    length, lanes = q_ref.shape
    half, heads = 64, lanes // 64
    wide = jnp.float32
    for block in range(length // KEYS):
        part = pl.ds(block * KEYS, KEYS)
        km_ref[0, part, :], km_ref[1, part, :] = one_head(k_ref[part, :], half)
        vt_ref[block] = flipped(v_ref[part, :]).astype(jnp.bfloat16)

    for block in range(length // ROWS):
        rows = pl.ds(block * ROWS, ROWS)
        queries = q_ref[rows, :] * jnp.bfloat16(half**-0.5)
        row_docs = seg_row_ref[:, rows]

        def step(index, carry, queries=queries, row_docs=row_docs):
            part = pl.ds(pl.multiple_of(index * KEYS, KEYS), KEYS)
            docs = seg_col_ref[part, :]
            key_docs = jnp.concatenate([docs] * (ROWS // 128), axis=1)
            every = range(heads)
            pairs = [slice(head // 2 * 128, head // 2 * 128 + 128) for head in every]
            scores = [
                head_scores(km_ref[head % 2, part, pairs[head]], queries[:, pairs[head]], key_docs, row_docs)
                for head in every
            ]
            tops = [jnp.maximum(carry[h][0], jnp.max(scores[h], axis=0, keepdims=True)) for h in every]
            shrinks = [jnp.exp(carry[h][0] - tops[h]) for h in every]
            expos = [jnp.exp(scores[h] - tops[h]) for h in every]
            totals = [shrinks[h] * carry[h][1] + jnp.sum(expos[h], axis=0, keepdims=True) for h in every]
            values = [vt_ref[index, h * half : (h + 1) * half, :] for h in every]
            adds = [jnp.dot(values[h], expos[h].astype(jnp.bfloat16), preferred_element_type=wide) for h in every]
            new = [(tops[h], totals[h], shrinks[h] * carry[h][2] + adds[h]) for h in every]
            return tuple(new)

        start = tuple(
            (jnp.full((1, ROWS), -1000000000.0, wide), jnp.zeros((1, ROWS), wide), jnp.zeros((half, ROWS), wide))
            for _ in range(heads)
        )
        done = lax.fori_loop(lo_ref[block], hi_ref[block], step, start)
        mixed = jnp.concatenate([acc / total for _, total, acc in done], axis=0)
        out_ref[rows, :] = mixed.T.astype(out_ref.dtype)
        for head in range(heads):
            log_ref[0, head : head + 1, rows] = done[head][0] + jnp.log(done[head][1])


def attend_back_kernel(
    lo_ref, hi_ref, q_ref, k_ref, v_ref, grad_ref, mixed_ref, log_ref, seg_col_ref, seg_row_ref,
    dq_ref, dk_ref, dv_ref, km_ref, vm_ref, kt_ref, dk_acc, dv_acc,
):
    length, lanes = q_ref.shape
    half, heads = 64, lanes // 64
    wide, low = jnp.float32, jnp.bfloat16
    scale = half**-0.5
    for block in range(length // KEYS):
        part = pl.ds(block * KEYS, KEYS)
        km_ref[0, part, :], km_ref[1, part, :] = one_head(k_ref[part, :], half)
        vm_ref[0, part, :], vm_ref[1, part, :] = one_head(v_ref[part, :], half)
        kt_ref[block] = flipped(k_ref[part, :]).astype(low)
    dk_acc[...] = jnp.zeros_like(dk_acc)
    dv_acc[...] = jnp.zeros_like(dv_acc)

    for block in range(length // ROWS):
        rows = pl.ds(block * ROWS, ROWS)
        queries = q_ref[rows, :] * low(scale)
        grads = grad_ref[rows, :]
        row_docs = seg_row_ref[:, rows]
        queries_both = jnp.concatenate(one_head(queries, half), axis=0)
        grads_both = jnp.concatenate(one_head(grads, half), axis=0)
        products = (grads.astype(wide) * mixed_ref[rows, :].astype(wide)).T
        dots = [jnp.sum(products[h * half : (h + 1) * half], axis=0, keepdims=True) for h in range(heads)]
        logs = [log_ref[0, h : h + 1, rows] for h in range(heads)]

        def step(index, carry):
            part = pl.ds(pl.multiple_of(index * KEYS, KEYS), KEYS)
            docs = seg_col_ref[part, :]
            key_docs = jnp.concatenate([docs] * (ROWS // 128), axis=1)
            every = range(heads)
            pairs = [slice(h // 2 * 128, h // 2 * 128 + 128) for h in every]
            scores = [
                head_scores(km_ref[h % 2, part, pairs[h]], queries[:, pairs[h]], key_docs, row_docs) for h in every
            ]
            grad_probs = [
                lax.dot_general(vm_ref[h % 2, part, pairs[h]], grads[:, pairs[h]], NT, preferred_element_type=wide)
                for h in every
            ]
            probs = [jnp.exp(scores[h] - logs[h]) for h in every]
            slopes = [(probs[h] * (grad_probs[h] - dots[h])).astype(low) for h in every]
            keys = [kt_ref[index, h * half : (h + 1) * half, :] for h in every]
            new = [carry[h] + jnp.dot(keys[h], slopes[h], preferred_element_type=wide) for h in every]
            for h in range(0, heads, 2):
                dv_acc[part, pairs[h]] += jnp.dot(
                    jnp.concatenate([probs[h].astype(low), probs[h + 1].astype(low)], axis=1),
                    grads_both[:, pairs[h]],
                    preferred_element_type=wide,
                )
                dk_acc[part, pairs[h]] += jnp.dot(
                    jnp.concatenate(slopes[h : h + 2], axis=1), queries_both[:, pairs[h]], preferred_element_type=wide
                )
            return tuple(new)

        zero = jnp.zeros((half, ROWS), wide)
        dq = lax.fori_loop(lo_ref[block], hi_ref[block], step, (zero,) * heads)
        dq_ref[rows, :] = (jnp.concatenate(dq, axis=0).T * scale).astype(low)
    dk_ref[...] = dk_acc[...].astype(low)
    dv_ref[...] = dv_acc[...].astype(low)


def key_ranges(doc_ids):
    ends = doc_ids.reshape(-1, ROWS)
    lo = jnp.sum(doc_ids[None, :] < ends[:, :1], axis=1, dtype=jnp.int32) // KEYS
    hi = (jnp.sum(doc_ids[None, :] <= ends[:, -1:], axis=1, dtype=jnp.int32) + KEYS - 1) // KEYS
    return lo, hi


def attend(qkv, docs):
    lo, hi, seg_col, seg_row = docs
    length = qkv.shape[0]
    width = qkv.shape[1] // 3
    lanes = PAIRS * 128
    pairs = width // lanes
    column = lambda base: pl.BlockSpec((length, lanes), lambda i, *_: (0, base * pairs + i))
    whole = lambda shape: pl.BlockSpec(shape, lambda i, *_: (0, 0))
    return pl.pallas_call(
        attend_kernel,
        grid_spec=pltpu.PrefetchScalarGridSpec(
            num_scalar_prefetch=2,
            grid=(pairs,),
            in_specs=[column(0), column(1), column(2), whole((length, 128)), whole((1, length))],
            out_specs=[column(0), pl.BlockSpec((1, 16, length), lambda i, *_: (i, 0, 0))],
            scratch_shapes=[
                pltpu.VMEM((2, length, lanes), jnp.bfloat16),
                pltpu.VMEM((length // KEYS, lanes, KEYS), jnp.bfloat16),
            ],
        ),
        out_shape=[
            jax.ShapeDtypeStruct((length, width), jnp.bfloat16),
            jax.ShapeDtypeStruct((pairs, 16, length), jnp.float32),
        ],
        name="attend",
    )(lo, hi, qkv, qkv, qkv, seg_col, seg_row)


def attend_back(qkv, grad, mixed, logs, docs):
    lo, hi, seg_col, seg_row = docs
    length = qkv.shape[0]
    width = qkv.shape[1] // 3
    lanes = PAIRS * 128
    pairs = width // lanes
    column = lambda base: pl.BlockSpec((length, lanes), lambda i, *_: (0, base * pairs + i))
    whole = lambda shape: pl.BlockSpec(shape, lambda i, *_: (0, 0))
    return pl.pallas_call(
        attend_back_kernel,
        grid_spec=pltpu.PrefetchScalarGridSpec(
            num_scalar_prefetch=2,
            grid=(pairs,),
            in_specs=[column(0), column(1), column(2), column(0), column(0),
                pl.BlockSpec((1, 16, length), lambda i, *_: (i, 0, 0)), whole((length, 128)), whole((1, length))],
            out_specs=[column(0)] * 3,
            scratch_shapes=[
                pltpu.VMEM((2, length, lanes), jnp.bfloat16),
                pltpu.VMEM((2, length, lanes), jnp.bfloat16),
                pltpu.VMEM((length // KEYS, lanes, KEYS), jnp.bfloat16),
                pltpu.VMEM((length, lanes), jnp.float32),
                pltpu.VMEM((length, lanes), jnp.float32),
            ],
        ),
        out_shape=[jax.ShapeDtypeStruct((length, width), jnp.bfloat16)] * 3,
        name="attend_back",
    )(lo, hi, qkv, qkv, qkv, grad, mixed, logs, seg_col, seg_row)


def doc_tables(doc_ids):
    lo, hi = key_ranges(doc_ids)
    return lo, hi, jnp.broadcast_to(doc_ids[:, None], (doc_ids.shape[0], 128)), doc_ids[None, :]

def gelu_parts(pre):
    size = jnp.abs(pre) * (0.5**0.5)
    square = size * size
    t = 1.0 / (1.0 + 0.5 * size)
    series = 0.17087277
    for term in (-0.82215223, 1.48851587, -1.13520398, 0.27886807, -0.18628806, 0.09678418, 0.37409196, 1.00002368, -1.26551223):
        series = term + t * series
    tail = 0.5 * t * jnp.exp(series - square)
    below = jnp.where(pre >= 0, 1.0 - tail, tail)
    return pre * below, below + pre * jnp.exp(-square) * ((2.0 * jnp.pi) ** -0.5)


def layer_norm(resid, gain, shift):
    row_mean = jnp.mean(resid, axis=-1, keepdims=True)
    centred = resid - row_mean
    variance = jnp.mean(centred * centred, axis=-1, keepdims=True)
    inv_std = lax.rsqrt(variance + 1e-05)
    normed = centred * inv_std
    return (normed * gain + shift, normed, inv_std)


def norm_back(grad_in, gain, normed, inv_std):
    grad_norm = grad_in * gain
    first = jnp.mean(grad_norm, axis=-1, keepdims=True)
    second = jnp.mean(grad_norm * normed, axis=-1, keepdims=True)
    return inv_std * (grad_norm - first - normed * second)


def project(left, weight, bias):
    return jnp.dot(left, weight, preferred_element_type=jnp.float32) + bias.astype(jnp.float32)


def weight_grad(left, right):
    return jnp.einsum("ti,to->io", left, right, preferred_element_type=jnp.float32)


def back_input(grad_rows, weight):
    return jnp.einsum("to,io->ti", grad_rows, weight, preferred_element_type=jnp.float32)


def col_sum(values):
    return jnp.sum(values.astype(jnp.float32), axis=0)


def owner_blocks(matrices, vectors):
    devices = lax.axis_size("dp")
    width = matrices[0].shape[1]
    pieces, shapes = [], []
    for matrix in matrices:
        low = matrix.astype(jnp.bfloat16)
        own = low.shape[0] // devices
        blocks = low.reshape(devices, own, low.shape[1])
        parts = low.shape[1] // width
        pieces += [blocks[:, :, i * width : (i + 1) * width] for i in range(parts)]
        shapes.append((own, parts))
    flat = [vector.reshape(devices, -1) for vector in vectors]
    lengths = [vector.shape[1] for vector in flat]
    packed = jnp.concatenate(flat, axis=1)
    packed = jnp.pad(packed, ((0, 0), (0, 8 * width - packed.shape[1])))
    pieces.append(packed.reshape(devices, 8, width).astype(jnp.bfloat16))
    return jnp.concatenate(pieces, axis=1), (shapes, lengths)


def own_shares(mine, layout):
    shapes, lengths = layout
    mine = mine.astype(jnp.float32)
    outs, at = [], 0
    for own, parts in shapes:
        outs.append(
            jnp.concatenate([mine[at + i * own : at + (i + 1) * own] for i in range(parts)], axis=1)
        )
        at += own * parts
    tail, at = mine[at:].reshape(-1), 0
    for length in lengths:
        outs.append(tail[at : at + length])
        at += length
    return tuple(outs)


def plane_sum(blocks):
    devices = lax.axis_size("dp")
    runs = devices // PLANE
    if devices % PLANE or runs < 2:
        return lax.psum_scatter(blocks, "dp", scatter_dimension=0, tiled=True)[0]
    inner = [[run * PLANE + i for i in range(PLANE)] for run in range(runs)]
    outer = [[run * PLANE + i for run in range(runs)] for i in range(PLANE)]
    part = lax.psum_scatter(blocks, "dp", scatter_dimension=0, tiled=True, axis_index_groups=inner)
    return lax.psum_scatter(part, "dp", scatter_dimension=0, tiled=True, axis_index_groups=outer)[0]


def plane_order(blocks):
    devices = blocks.shape[0]
    if devices % PLANE or devices == PLANE:
        return blocks
    parts = blocks.reshape((devices // PLANE, PLANE) + blocks.shape[1:])
    return parts.swapaxes(0, 1).reshape(blocks.shape)


def halve(blocks, bit, left):
    devices = lax.axis_size("dp")
    low_count = 2 ** left.index(bit)
    view = blocks.reshape((blocks.shape[0] // (2 * low_count), 2, low_count) + blocks.shape[1:])
    mine = (lax.axis_index("dp") >> bit) & 1
    kept = lax.dynamic_index_in_dim(view, mine, 1, keepdims=False)
    sent = lax.dynamic_index_in_dim(view, 1 - mine, 1, keepdims=False)
    got = lax.ppermute(sent, "dp", [(i, i ^ (1 << bit)) for i in range(devices)])
    added = (kept.astype(jnp.float32) + got.astype(jnp.float32)).astype(blocks.dtype)
    return added.reshape((-1,) + blocks.shape[1:]), [b for b in left if b != bit]


def halving_sum(blocks):
    devices = lax.axis_size("dp")
    if devices & (devices - 1) or devices < 8:
        return lax.psum_scatter(blocks, "dp", scatter_dimension=0, tiled=True)[0]
    left = list(range(devices.bit_length() - 1))
    blocks, left = halve(blocks, 0, left)
    middle = blocks.shape[1] // 16 * 8
    one, two = blocks[:, :middle], blocks[:, middle:]
    one, one_left = halve(one, 1, left)
    two, two_left = halve(two, 2, left)
    one, one_left = halve(one, 2, one_left)
    two, two_left = halve(two, 1, two_left)
    blocks, left = jnp.concatenate([one, two], axis=1), one_left
    for bit in list(left):
        blocks, left = halve(blocks, bit, left)
    return blocks[0]


def shards(
    layer_input,
    segments,
    cotangent,
    w_query,
    b_query,
    w_key,
    w_value,
    b_value,
    w_out,
    b_out,
    norm1_gain,
    norm1_bias,
    w_in,
    b_in,
    w_down,
    b_down,
    norm2_gain,
    norm2_bias,
):
    low_type = jnp.bfloat16
    wide_type = jnp.float32
    own_rows, width = w_query.shape
    hidden = w_in.shape[1]
    fold = hidden // width
    devices = lax.axis_size("dp")
    vectors = (b_query, b_value, b_out, norm1_gain, norm1_bias, b_down, norm2_gain, norm2_bias)
    columns = jnp.concatenate([jnp.stack(vectors, axis=1), b_in.reshape(own_rows, fold)], axis=1)
    columns = jnp.pad(columns, ((0, 0), (0, 128 - columns.shape[1])))
    down_parts = [w_down[i * own_rows : (i + 1) * own_rows] for i in range(fold)]
    packed = jnp.concatenate([w_query, w_key, w_value, columns, w_out, w_in] + down_parts, axis=1)
    gathered = lax.all_gather(packed, "dp", axis=0, tiled=True)
    full_qkv = gathered[:, : 3 * width]
    full_columns = gathered[:, 3 * width : 3 * width + 128]
    at = 3 * width + 128
    full_wo = gathered[:, at : at + width]
    full_win = gathered[:, at + width : at + width + hidden]
    full_wdown = gathered[:, at + width + hidden :].reshape(devices, own_rows, fold, width)
    full_wdown = full_wdown.swapaxes(1, 2).reshape(hidden, width)
    vector_rows = full_columns.T.astype(wide_type)
    full_bq, full_bv, full_bo, gain_one, shift_one, full_bdown, gain_two, shift_two = (
        vector_rows[i] for i in range(8)
    )
    full_bin = full_columns[:, 8 : 8 + fold].astype(wide_type).reshape(-1)

    tokens = layer_input[0]
    docs = doc_tables(segments[0])
    bias = jnp.concatenate([full_bq, jnp.zeros_like(full_bq), full_bv])
    qkv = project(tokens, full_qkv, bias).astype(low_type)
    context, log_total = attend(qkv, docs)
    resid_one = tokens.astype(wide_type) + project(context, full_wo, full_bo)
    hidden_one, normed_one, inv_one = layer_norm(resid_one, gain_one, shift_one)
    hidden_low = hidden_one.astype(low_type)
    activated, slope = gelu_parts(project(hidden_low, full_win, full_bin))
    act_low, slope = activated.astype(low_type), slope.astype(low_type)
    resid_two = hidden_one + project(act_low, full_wdown, full_bdown)
    outputs, normed_two, inv_two = layer_norm(resid_two, gain_two, shift_two)
    layer_out = outputs.astype(low_type)[None]

    grad_out = cotangent[0].astype(wide_type)
    grad_gain_two = jnp.sum(grad_out * normed_two, axis=0)
    grad_shift_two = jnp.sum(grad_out, axis=0)
    grad_resid_two = norm_back(grad_out, gain_two, normed_two, inv_two)
    grad_ffn = grad_resid_two.astype(low_type)
    grad_bdown = col_sum(grad_ffn)
    grad_wdown = weight_grad(act_low, grad_ffn)
    grad_pre = (back_input(grad_ffn, full_wdown) * slope.astype(wide_type)).astype(low_type)
    grad_bin = col_sum(grad_pre)
    grad_win = weight_grad(hidden_low, grad_pre)
    grad_hidden = grad_resid_two + back_input(grad_pre, full_win)
    grad_gain_one = jnp.sum(grad_hidden * normed_one, axis=0)
    grad_shift_one = jnp.sum(grad_hidden, axis=0)
    grad_resid_one = norm_back(grad_hidden, gain_one, normed_one, inv_one)
    grad_attn = grad_resid_one.astype(low_type)
    grad_bo = col_sum(grad_attn)
    grad_wo = weight_grad(context, grad_attn)
    ffn_blocks, ffn_layout = owner_blocks(
        (grad_wo, grad_win, grad_wdown),
        (grad_bo, grad_gain_one, grad_shift_one, grad_bin, grad_bdown, grad_gain_two, grad_shift_two),
    )
    ffn_blocks = plane_order(ffn_blocks)
    grad_context = back_input(grad_attn, full_wo).astype(low_type)
    ffn_blocks, grad_context = lax.optimization_barrier((ffn_blocks, grad_context))
    ffn_mine = plane_sum(ffn_blocks)

    grad_query, grad_key, grad_value = attend_back(qkv, grad_context, context, log_total, docs)
    attn_blocks, attn_layout = owner_blocks(
        tuple(weight_grad(tokens, grad) for grad in (grad_query, grad_key, grad_value)),
        (col_sum(grad_query), col_sum(grad_value)),
    )
    attn_mine = halving_sum(attn_blocks)
    grad_tokens = (
        grad_resid_one
        + back_input(grad_query, full_qkv[:, :width])
        + back_input(grad_key, full_qkv[:, width : 2 * width])
        + back_input(grad_value, full_qkv[:, 2 * width :])
    )
    own_wq, own_wk, own_wv, own_bq, own_bv = own_shares(attn_mine, attn_layout)
    (
        own_wo,
        own_win,
        own_wdown,
        own_bo,
        own_gain_one,
        own_shift_one,
        own_bin,
        own_bdown,
        own_gain_two,
        own_shift_two,
    ) = own_shares(ffn_mine, ffn_layout)
    return (
        layer_out,
        grad_tokens[None],
        own_wq,
        own_bq,
        own_wk,
        own_wv,
        own_bv,
        own_wo,
        own_bo,
        own_gain_one,
        own_shift_one,
        own_win,
        own_bin,
        own_wdown,
        own_bdown,
        own_gain_two,
        own_shift_two,
    )


def solution(mesh):
    placed = (
        P("dp", None, None),
        P("dp", None),
        P("dp", None, None),
        P("dp", None),
        P("dp"),
        P("dp", None),
        P("dp", None),
        P("dp"),
        P("dp", None),
        P("dp"),
        P("dp"),
        P("dp"),
        P("dp", None),
        P("dp"),
        P("dp", None),
        P("dp"),
        P("dp"),
        P("dp"),
    )
    return jax.shard_map(
        shards,
        mesh=mesh,
        in_specs=placed,
        out_specs=(
            P("dp", None, None),
            P("dp", None, None),
            P("dp", None),
            P("dp"),
            P("dp", None),
            P("dp", None),
            P("dp"),
            P("dp", None),
            P("dp"),
            P("dp"),
            P("dp"),
            P("dp", None),
            P("dp"),
            P("dp", None),
            P("dp"),
            P("dp"),
            P("dp"),
        ),
        check_vma=False,
    )
```

```python
import jax
import jax.numpy as jnp
from jax import lax
from jax.experimental import pallas as pl
from jax.experimental.pallas import tpu as pltpu
from jax.sharding import PartitionSpec as P

HEADS = 12
ROWS = 256
KEYS = 256
PAIRS = 3
PLANE = 8

NT = (((1,), (1,)), ((), ()))


def flipped(values):
    return values.astype(jnp.float32).T


def one_head(values, half):
    lane = lax.broadcasted_iota(jnp.int32, values.shape, 1) % (2 * half)
    return jnp.where(lane < half, values, 0), jnp.where(lane >= half, values, 0)


def head_scores(keys, queries, key_docs, row_docs):
    raw = lax.dot_general(keys, queries, NT, preferred_element_type=jnp.float32)
    return jnp.where(key_docs == row_docs, raw, -1000000000.0)


def attend_kernel(lo_ref, hi_ref, q_ref, k_ref, v_ref, seg_col_ref, seg_row_ref, out_ref, log_ref, km_ref, vt_ref):
    length, lanes = q_ref.shape
    half, heads = 64, lanes // 64
    wide = jnp.float32
    for block in range(length // KEYS):
        part = pl.ds(block * KEYS, KEYS)
        km_ref[0, part, :], km_ref[1, part, :] = one_head(k_ref[part, :], half)
        vt_ref[block] = flipped(v_ref[part, :]).astype(jnp.bfloat16)

    for block in range(length // ROWS):
        rows = pl.ds(block * ROWS, ROWS)
        queries = q_ref[rows, :] * jnp.bfloat16(half**-0.5)
        row_docs = seg_row_ref[:, rows]

        def step(index, carry, queries=queries, row_docs=row_docs):
            part = pl.ds(pl.multiple_of(index * KEYS, KEYS), KEYS)
            docs = seg_col_ref[part, :]
            key_docs = jnp.concatenate([docs] * (ROWS // 128), axis=1)
            every = range(heads)
            pairs = [slice(head // 2 * 128, head // 2 * 128 + 128) for head in every]
            scores = [
                head_scores(km_ref[head % 2, part, pairs[head]], queries[:, pairs[head]], key_docs, row_docs)
                for head in every
            ]
            tops = [jnp.maximum(carry[h][0], jnp.max(scores[h], axis=0, keepdims=True)) for h in every]
            shrinks = [jnp.exp(carry[h][0] - tops[h]) for h in every]
            expos = [jnp.exp(scores[h] - tops[h]) for h in every]
            totals = [shrinks[h] * carry[h][1] + jnp.sum(expos[h], axis=0, keepdims=True) for h in every]
            values = [vt_ref[index, h * half : (h + 1) * half, :] for h in every]
            adds = [jnp.dot(values[h], expos[h].astype(jnp.bfloat16), preferred_element_type=wide) for h in every]
            new = [(tops[h], totals[h], shrinks[h] * carry[h][2] + adds[h]) for h in every]
            return tuple(new)

        start = tuple(
            (jnp.full((1, ROWS), -1000000000.0, wide), jnp.zeros((1, ROWS), wide), jnp.zeros((half, ROWS), wide))
            for _ in range(heads)
        )
        done = lax.fori_loop(lo_ref[block], hi_ref[block], step, start)
        mixed = jnp.concatenate([acc / total for _, total, acc in done], axis=0)
        out_ref[rows, :] = mixed.T.astype(out_ref.dtype)
        for head in range(heads):
            log_ref[0, head : head + 1, rows] = done[head][0] + jnp.log(done[head][1])


def attend_back_kernel(
    lo_ref, hi_ref, q_ref, k_ref, v_ref, grad_ref, mixed_ref, log_ref, seg_col_ref, seg_row_ref,
    dq_ref, dk_ref, dv_ref, km_ref, vm_ref, kt_ref, dk_acc, dv_acc,
):
    length, lanes = q_ref.shape
    half, heads = 64, lanes // 64
    wide, low = jnp.float32, jnp.bfloat16
    scale = half**-0.5
    for block in range(length // KEYS):
        part = pl.ds(block * KEYS, KEYS)
        km_ref[0, part, :], km_ref[1, part, :] = one_head(k_ref[part, :], half)
        vm_ref[0, part, :], vm_ref[1, part, :] = one_head(v_ref[part, :], half)
        kt_ref[block] = flipped(k_ref[part, :]).astype(low)
    dk_acc[...] = jnp.zeros_like(dk_acc)
    dv_acc[...] = jnp.zeros_like(dv_acc)

    for block in range(length // ROWS):
        rows = pl.ds(block * ROWS, ROWS)
        queries = q_ref[rows, :] * low(scale)
        grads = grad_ref[rows, :]
        row_docs = seg_row_ref[:, rows]
        queries_both = jnp.concatenate(one_head(queries, half), axis=0)
        grads_both = jnp.concatenate(one_head(grads, half), axis=0)
        products = (grads.astype(wide) * mixed_ref[rows, :].astype(wide)).T
        dots = [jnp.sum(products[h * half : (h + 1) * half], axis=0, keepdims=True) for h in range(heads)]
        logs = [log_ref[0, h : h + 1, rows] for h in range(heads)]

        def step(index, carry):
            part = pl.ds(pl.multiple_of(index * KEYS, KEYS), KEYS)
            docs = seg_col_ref[part, :]
            key_docs = jnp.concatenate([docs] * (ROWS // 128), axis=1)
            every = range(heads)
            pairs = [slice(h // 2 * 128, h // 2 * 128 + 128) for h in every]
            scores = [
                head_scores(km_ref[h % 2, part, pairs[h]], queries[:, pairs[h]], key_docs, row_docs) for h in every
            ]
            grad_probs = [
                lax.dot_general(vm_ref[h % 2, part, pairs[h]], grads[:, pairs[h]], NT, preferred_element_type=wide)
                for h in every
            ]
            probs = [jnp.exp(scores[h] - logs[h]) for h in every]
            slopes = [(probs[h] * (grad_probs[h] - dots[h])).astype(low) for h in every]
            keys = [kt_ref[index, h * half : (h + 1) * half, :] for h in every]
            new = [carry[h] + jnp.dot(keys[h], slopes[h], preferred_element_type=wide) for h in every]
            for h in range(0, heads, 2):
                dv_acc[part, pairs[h]] += jnp.dot(
                    jnp.concatenate([probs[h].astype(low), probs[h + 1].astype(low)], axis=1),
                    grads_both[:, pairs[h]],
                    preferred_element_type=wide,
                )
                dk_acc[part, pairs[h]] += jnp.dot(
                    jnp.concatenate(slopes[h : h + 2], axis=1), queries_both[:, pairs[h]], preferred_element_type=wide
                )
            return tuple(new)

        zero = jnp.zeros((half, ROWS), wide)
        dq = lax.fori_loop(lo_ref[block], hi_ref[block], step, (zero,) * heads)
        dq_ref[rows, :] = (jnp.concatenate(dq, axis=0).T * scale).astype(low)
    dk_ref[...] = dk_acc[...].astype(low)
    dv_ref[...] = dv_acc[...].astype(low)


def key_ranges(doc_ids):
    ends = doc_ids.reshape(-1, ROWS)
    lo = jnp.sum(doc_ids[None, :] < ends[:, :1], axis=1, dtype=jnp.int32) // KEYS
    hi = (jnp.sum(doc_ids[None, :] <= ends[:, -1:], axis=1, dtype=jnp.int32) + KEYS - 1) // KEYS
    return lo, hi


def attend(qkv, docs):
    lo, hi, seg_col, seg_row = docs
    length = qkv.shape[0]
    width = qkv.shape[1] // 3
    lanes = PAIRS * 128
    pairs = width // lanes
    column = lambda base: pl.BlockSpec((length, lanes), lambda i, *_: (0, base * pairs + i))
    whole = lambda shape: pl.BlockSpec(shape, lambda i, *_: (0, 0))
    return pl.pallas_call(
        attend_kernel,
        grid_spec=pltpu.PrefetchScalarGridSpec(
            num_scalar_prefetch=2,
            grid=(pairs,),
            in_specs=[column(0), column(1), column(2), whole((length, 128)), whole((1, length))],
            out_specs=[column(0), pl.BlockSpec((1, 16, length), lambda i, *_: (i, 0, 0))],
            scratch_shapes=[
                pltpu.VMEM((2, length, lanes), jnp.bfloat16),
                pltpu.VMEM((length // KEYS, lanes, KEYS), jnp.bfloat16),
            ],
        ),
        out_shape=[
            jax.ShapeDtypeStruct((length, width), jnp.bfloat16),
            jax.ShapeDtypeStruct((pairs, 16, length), jnp.float32),
        ],
        name="attend",
    )(lo, hi, qkv, qkv, qkv, seg_col, seg_row)


def attend_back(qkv, grad, mixed, logs, docs):
    lo, hi, seg_col, seg_row = docs
    length = qkv.shape[0]
    width = qkv.shape[1] // 3
    lanes = PAIRS * 128
    pairs = width // lanes
    column = lambda base: pl.BlockSpec((length, lanes), lambda i, *_: (0, base * pairs + i))
    whole = lambda shape: pl.BlockSpec(shape, lambda i, *_: (0, 0))
    return pl.pallas_call(
        attend_back_kernel,
        grid_spec=pltpu.PrefetchScalarGridSpec(
            num_scalar_prefetch=2,
            grid=(pairs,),
            in_specs=[column(0), column(1), column(2), column(0), column(0),
                pl.BlockSpec((1, 16, length), lambda i, *_: (i, 0, 0)), whole((length, 128)), whole((1, length))],
            out_specs=[column(0)] * 3,
            scratch_shapes=[
                pltpu.VMEM((2, length, lanes), jnp.bfloat16),
                pltpu.VMEM((2, length, lanes), jnp.bfloat16),
                pltpu.VMEM((length // KEYS, lanes, KEYS), jnp.bfloat16),
                pltpu.VMEM((length, lanes), jnp.float32),
                pltpu.VMEM((length, lanes), jnp.float32),
            ],
        ),
        out_shape=[jax.ShapeDtypeStruct((length, width), jnp.bfloat16)] * 3,
        name="attend_back",
    )(lo, hi, qkv, qkv, qkv, grad, mixed, logs, seg_col, seg_row)


def doc_tables(doc_ids):
    lo, hi = key_ranges(doc_ids)
    return lo, hi, jnp.broadcast_to(doc_ids[:, None], (doc_ids.shape[0], 128)), doc_ids[None, :]

def gelu_parts(pre):
    size = jnp.abs(pre) * (0.5**0.5)
    square = size * size
    t = 1.0 / (1.0 + 0.5 * size)
    series = 0.17087277
    for term in (-0.82215223, 1.48851587, -1.13520398, 0.27886807, -0.18628806, 0.09678418, 0.37409196, 1.00002368, -1.26551223):
        series = term + t * series
    tail = 0.5 * t * jnp.exp(series - square)
    below = jnp.where(pre >= 0, 1.0 - tail, tail)
    return pre * below, below + pre * jnp.exp(-square) * ((2.0 * jnp.pi) ** -0.5)


def layer_norm(resid, gain, shift):
    row_mean = jnp.mean(resid, axis=-1, keepdims=True)
    centred = resid - row_mean
    variance = jnp.mean(centred * centred, axis=-1, keepdims=True)
    inv_std = lax.rsqrt(variance + 1e-05)
    normed = centred * inv_std
    return (normed * gain + shift, normed, inv_std)


def norm_back(grad_in, gain, normed, inv_std):
    grad_norm = grad_in * gain
    first = jnp.mean(grad_norm, axis=-1, keepdims=True)
    second = jnp.mean(grad_norm * normed, axis=-1, keepdims=True)
    return inv_std * (grad_norm - first - normed * second)


def project(left, weight, bias):
    return jnp.dot(left, weight, preferred_element_type=jnp.float32) + bias.astype(jnp.float32)


def weight_grad(left, right):
    return jnp.einsum("ti,to->io", left, right, preferred_element_type=jnp.float32)


def back_input(grad_rows, weight):
    return jnp.einsum("to,io->ti", grad_rows, weight, preferred_element_type=jnp.float32)


def col_sum(values):
    return jnp.sum(values.astype(jnp.float32), axis=0)


def owner_blocks(matrices, vectors):
    devices = lax.axis_size("dp")
    width = matrices[0].shape[1]
    pieces, shapes = [], []
    for matrix in matrices:
        low = matrix.astype(jnp.bfloat16)
        own = low.shape[0] // devices
        blocks = low.reshape(devices, own, low.shape[1])
        parts = low.shape[1] // width
        pieces += [blocks[:, :, i * width : (i + 1) * width] for i in range(parts)]
        shapes.append((own, parts))
    if not vectors:
        return jnp.concatenate(pieces, axis=1), (shapes, [])
    flat = [vector.reshape(devices, -1) for vector in vectors]
    lengths = [vector.shape[1] for vector in flat]
    packed = jnp.concatenate(flat, axis=1)
    packed = jnp.pad(packed, ((0, 0), (0, 8 * width - packed.shape[1])))
    pieces.append(packed.reshape(devices, 8, width).astype(jnp.bfloat16))
    return jnp.concatenate(pieces, axis=1), (shapes, lengths)


def own_shares(mine, layout):
    shapes, lengths = layout
    mine = mine.astype(jnp.float32)
    outs, at = [], 0
    for own, parts in shapes:
        outs.append(
            jnp.concatenate([mine[at + i * own : at + (i + 1) * own] for i in range(parts)], axis=1)
        )
        at += own * parts
    tail, at = mine[at:].reshape(-1), 0
    for length in lengths:
        outs.append(tail[at : at + length])
        at += length
    return tuple(outs)


def plane_groups():
    devices = lax.axis_size("dp")
    runs = devices // PLANE
    if devices % PLANE or runs < 2:
        return None
    inner = [[run * PLANE + i for i in range(PLANE)] for run in range(runs)]
    return inner, [[run * PLANE + i for run in range(runs)] for i in range(PLANE)]


def scatter(blocks, stage):
    groups = plane_groups()
    if groups is None:
        return blocks if stage else lax.psum_scatter(blocks, "dp", scatter_dimension=0, tiled=True)
    return lax.psum_scatter(blocks, "dp", scatter_dimension=0, tiled=True, axis_index_groups=groups[stage])


def plane_order(blocks):
    devices = blocks.shape[0]
    if devices % PLANE or devices == PLANE:
        return blocks
    parts = blocks.reshape((devices // PLANE, PLANE) + blocks.shape[1:])
    return parts.swapaxes(0, 1).reshape(blocks.shape)


def double(shards, bit, held):
    devices = lax.axis_size("dp")
    low_count = 2 ** sum(b < bit for b in held)
    view = shards.reshape((shards.shape[0] // low_count, 1, low_count) + shards.shape[1:])
    got = lax.ppermute(view, "dp", [(i, i ^ (1 << bit)) for i in range(devices)])
    upper = ((lax.axis_index("dp") >> bit) & 1) == 1
    both = jnp.concatenate([jnp.where(upper, got, view), jnp.where(upper, view, got)], axis=1)
    return both.reshape((-1,) + shards.shape[1:]), held + [bit]


def doubling_gather(shard):
    devices = lax.axis_size("dp")
    if devices & (devices - 1) or devices < 8:
        return lax.all_gather(shard, "dp", axis=0, tiled=True)
    shards, held = shard[None], []
    for bit in range(3, devices.bit_length() - 1):
        shards, held = double(shards, bit, held)
    middle = shard.shape[1] // 256 * 128
    one, two = shards[:, :, :middle], shards[:, :, middle:]
    one, one_held = double(one, 2, held)
    two, two_held = double(two, 1, held)
    one, one_held = double(one, 1, one_held)
    two, two_held = double(two, 2, two_held)
    one, _ = double(one, 0, one_held)
    two, _ = double(two, 0, two_held)
    return jnp.concatenate([one, two], axis=2).reshape(-1, shard.shape[1])


def halve(blocks, bit, left):
    devices = lax.axis_size("dp")
    low_count = 2 ** left.index(bit)
    view = blocks.reshape((blocks.shape[0] // (2 * low_count), 2, low_count) + blocks.shape[1:])
    mine = (lax.axis_index("dp") >> bit) & 1
    kept = lax.dynamic_index_in_dim(view, mine, 1, keepdims=False)
    sent = lax.dynamic_index_in_dim(view, 1 - mine, 1, keepdims=False)
    got = lax.ppermute(sent, "dp", [(i, i ^ (1 << bit)) for i in range(devices)])
    added = (kept.astype(jnp.float32) + got.astype(jnp.float32)).astype(blocks.dtype)
    return added.reshape((-1,) + blocks.shape[1:]), [b for b in left if b != bit]


def halving_sum(blocks):
    devices = lax.axis_size("dp")
    if devices & (devices - 1) or devices < 8:
        return lax.psum_scatter(blocks, "dp", scatter_dimension=0, tiled=True)[0]
    left = list(range(devices.bit_length() - 1))
    blocks, left = halve(blocks, 0, left)
    middle = blocks.shape[1] // 16 * 8
    one, two = blocks[:, :middle], blocks[:, middle:]
    one, one_left = halve(one, 1, left)
    two, two_left = halve(two, 2, left)
    one, one_left = halve(one, 2, one_left)
    two, two_left = halve(two, 1, two_left)
    blocks, left = jnp.concatenate([one, two], axis=1), one_left
    for bit in list(left):
        blocks, left = halve(blocks, bit, left)
    return blocks[0]


def shards(
    layer_input,
    segments,
    cotangent,
    w_query,
    b_query,
    w_key,
    w_value,
    b_value,
    w_out,
    b_out,
    norm1_gain,
    norm1_bias,
    w_in,
    b_in,
    w_down,
    b_down,
    norm2_gain,
    norm2_bias,
):
    low_type = jnp.bfloat16
    wide_type = jnp.float32
    own_rows, width = w_query.shape
    hidden = w_in.shape[1]
    fold = hidden // width
    vectors = (b_query, b_value, b_out, norm1_gain, norm1_bias, b_down, norm2_gain, norm2_bias)
    columns = jnp.concatenate([jnp.stack(vectors, axis=1), b_in.reshape(own_rows, fold)], axis=1)
    columns = jnp.pad(columns, ((0, 0), (0, 128 - columns.shape[1])))
    first = doubling_gather(jnp.concatenate([w_query, w_key, w_value, columns], axis=1))
    full_qkv, full_columns = first[:, : 3 * width], first[:, 3 * width :]
    in_parts = [w_in[:, i * width : (i + 1) * width] for i in range(fold)]
    packed = jnp.concatenate([w_out] + in_parts + [w_down], axis=0)
    gathered = lax.all_gather(packed[None], "dp", axis=0, tiled=True)
    pieces = [gathered[:, i * own_rows : (i + 1) * own_rows].reshape(width, width) for i in range(1 + fold)]
    full_wo, full_win = pieces[0], jnp.concatenate(pieces[1:], axis=1)
    full_wdown = gathered[:, (1 + fold) * own_rows :].reshape(hidden, width)
    vector_rows = full_columns.T.astype(wide_type)
    full_bq, full_bv, full_bo, gain_one, shift_one, full_bdown, gain_two, shift_two = (
        vector_rows[i] for i in range(8)
    )
    full_bin = full_columns[:, 8 : 8 + fold].astype(wide_type).reshape(-1)

    tokens = layer_input[0]
    docs = doc_tables(segments[0])
    bias = jnp.concatenate([full_bq, jnp.zeros_like(full_bq), full_bv])
    qkv = project(tokens, full_qkv, bias).astype(low_type)
    context, log_total = attend(qkv, docs)
    resid_one = tokens.astype(wide_type) + project(context, full_wo, full_bo)
    hidden_one, normed_one, inv_one = layer_norm(resid_one, gain_one, shift_one)
    hidden_low = hidden_one.astype(low_type)
    activated, slope = gelu_parts(project(hidden_low, full_win, full_bin))
    act_low, slope = lax.optimization_barrier((activated.astype(low_type), slope.astype(low_type)))
    resid_two = hidden_one + project(act_low, full_wdown, full_bdown)
    outputs, normed_two, inv_two = layer_norm(resid_two, gain_two, shift_two)
    layer_out = outputs.astype(low_type)[None]

    grad_out = cotangent[0].astype(wide_type)
    grad_gain_two = jnp.sum(grad_out * normed_two, axis=0)
    grad_shift_two = jnp.sum(grad_out, axis=0)
    grad_resid_two = norm_back(grad_out, gain_two, normed_two, inv_two)
    grad_ffn = grad_resid_two.astype(low_type)
    grad_bdown = col_sum(grad_ffn)
    down_blocks = owner_blocks((weight_grad(act_low, grad_ffn),), ())[0]
    down_blocks, grad_ffn = lax.optimization_barrier((plane_order(down_blocks), grad_ffn))
    down_part = scatter(down_blocks, 0)
    grad_pre = (back_input(grad_ffn, full_wdown) * slope.astype(wide_type)).astype(low_type)
    grad_bin = col_sum(grad_pre)
    grad_win = weight_grad(hidden_low, grad_pre)
    grad_hidden = grad_resid_two + back_input(grad_pre, full_win)
    grad_gain_one = jnp.sum(grad_hidden * normed_one, axis=0)
    grad_shift_one = jnp.sum(grad_hidden, axis=0)
    grad_resid_one = norm_back(grad_hidden, gain_one, normed_one, inv_one)
    grad_attn = grad_resid_one.astype(low_type)
    grad_bo = col_sum(grad_attn)
    grad_wo = weight_grad(context, grad_attn)
    ffn_blocks, ffn_layout = owner_blocks(
        (grad_wo, grad_win),
        (grad_bo, grad_gain_one, grad_shift_one, grad_bin, grad_bdown, grad_gain_two, grad_shift_two),
    )
    ffn_blocks = plane_order(ffn_blocks)
    grad_context = back_input(grad_attn, full_wo).astype(low_type)
    ffn_blocks, grad_context = lax.optimization_barrier((ffn_blocks, grad_context))
    ffn_part = scatter(ffn_blocks, 0)
    ffn_mine = scatter(jnp.concatenate([down_part, ffn_part], axis=1), 1)[0]
    own_down_rows = w_down.shape[0]

    grad_query, grad_key, grad_value = attend_back(qkv, grad_context, context, log_total, docs)
    attn_blocks, attn_layout = owner_blocks(
        tuple(weight_grad(tokens, grad) for grad in (grad_query, grad_key, grad_value)),
        (col_sum(grad_query), col_sum(grad_value)),
    )
    attn_mine = halving_sum(attn_blocks)
    grad_tokens = (
        grad_resid_one
        + back_input(grad_query, full_qkv[:, :width])
        + back_input(grad_key, full_qkv[:, width : 2 * width])
        + back_input(grad_value, full_qkv[:, 2 * width :])
    )
    own_wq, own_wk, own_wv, own_bq, own_bv = own_shares(attn_mine, attn_layout)
    (
        own_wo,
        own_win,
        own_bo,
        own_gain_one,
        own_shift_one,
        own_bin,
        own_bdown,
        own_gain_two,
        own_shift_two,
    ) = own_shares(ffn_mine[own_down_rows:], ffn_layout)
    own_wdown = ffn_mine[:own_down_rows].astype(wide_type)
    return (
        layer_out,
        grad_tokens[None],
        own_wq,
        own_bq,
        own_wk,
        own_wv,
        own_bv,
        own_wo,
        own_bo,
        own_gain_one,
        own_shift_one,
        own_win,
        own_bin,
        own_wdown,
        own_bdown,
        own_gain_two,
        own_shift_two,
    )


def solution(mesh):
    placed = (
        P("dp", None, None),
        P("dp", None),
        P("dp", None, None),
        P("dp", None),
        P("dp"),
        P("dp", None),
        P("dp", None),
        P("dp"),
        P("dp", None),
        P("dp"),
        P("dp"),
        P("dp"),
        P("dp", None),
        P("dp"),
        P("dp", None),
        P("dp"),
        P("dp"),
        P("dp"),
    )
    return jax.shard_map(
        shards,
        mesh=mesh,
        in_specs=placed,
        out_specs=(
            P("dp", None, None),
            P("dp", None, None),
            P("dp", None),
            P("dp"),
            P("dp", None),
            P("dp", None),
            P("dp"),
            P("dp", None),
            P("dp"),
            P("dp"),
            P("dp"),
            P("dp", None),
            P("dp"),
            P("dp", None),
            P("dp"),
            P("dp"),
            P("dp"),
        ),
        check_vma=False,
    )
```

```python
import math

import jax
import jax.numpy as jnp
from jax import lax
from jax.experimental import pallas as pl
from jax.experimental.pallas import tpu as pltpu
from jax.sharding import PartitionSpec as P

HEADS = 12
ROWS = 256
KEYS = 256
PAIRS = 6
PLANE = 8

NT = (((1,), (1,)), ((), ()))


def flipped(values):
    return values.astype(jnp.float32).T


def one_head(values, half):
    lane = lax.broadcasted_iota(jnp.int32, values.shape, 1) % (2 * half)
    return jnp.where(lane < half, values, 0), jnp.where(lane >= half, values, 0)


def head_scores(keys, queries, key_docs, row_docs):
    raw = lax.dot_general(keys, queries, NT, preferred_element_type=jnp.float32)
    return jnp.where(key_docs == row_docs, raw, -1000000000.0)


def attend_kernel(lo_ref, hi_ref, q_ref, k_ref, v_ref, seg_col_ref, seg_row_ref, out_ref, log_ref, km_ref, vt_ref):
    length, lanes = q_ref.shape
    half, heads = 64, lanes // 64
    wide = jnp.float32
    for block in range(length // KEYS):
        part = pl.ds(block * KEYS, KEYS)
        km_ref[0, part, :], km_ref[1, part, :] = one_head(k_ref[part, :], half)
        vt_ref[block] = flipped(v_ref[part, :]).astype(jnp.bfloat16)

    for block in range(length // ROWS):
        rows = pl.ds(block * ROWS, ROWS)
        queries = q_ref[rows, :] * jnp.bfloat16(half**-0.5)
        row_docs = seg_row_ref[:, rows]

        def step(index, carry, queries=queries, row_docs=row_docs):
            part = pl.ds(pl.multiple_of(index * KEYS, KEYS), KEYS)
            docs = seg_col_ref[part, :]
            key_docs = jnp.concatenate([docs] * (ROWS // 128), axis=1)
            every = range(heads)
            pairs = [slice(head // 2 * 128, head // 2 * 128 + 128) for head in every]
            scores = [
                head_scores(km_ref[head % 2, part, pairs[head]], queries[:, pairs[head]], key_docs, row_docs)
                for head in every
            ]
            tops = [jnp.maximum(carry[h][0], jnp.max(scores[h], axis=0, keepdims=True)) for h in every]
            shrinks = [jnp.exp(carry[h][0] - tops[h]) for h in every]
            expos = [jnp.exp(scores[h] - tops[h]) for h in every]
            totals = [shrinks[h] * carry[h][1] + jnp.sum(expos[h], axis=0, keepdims=True) for h in every]
            values = [vt_ref[index, h * half : (h + 1) * half, :] for h in every]
            adds = [jnp.dot(values[h], expos[h].astype(jnp.bfloat16), preferred_element_type=wide) for h in every]
            new = [(tops[h], totals[h], shrinks[h] * carry[h][2] + adds[h]) for h in every]
            return tuple(new)

        start = tuple(
            (jnp.full((1, ROWS), -1000000000.0, wide), jnp.zeros((1, ROWS), wide), jnp.zeros((half, ROWS), wide))
            for _ in range(heads)
        )
        done = lax.fori_loop(lo_ref[block], hi_ref[block], step, start)
        mixed = jnp.concatenate([acc / total for _, total, acc in done], axis=0)
        out_ref[rows, :] = mixed.T.astype(out_ref.dtype)
        for head in range(heads):
            log_ref[0, head : head + 1, rows] = done[head][0] + jnp.log(done[head][1])


def attend_back_kernel(
    lo_ref, hi_ref, q_ref, k_ref, v_ref, grad_ref, mixed_ref, log_ref, seg_col_ref, seg_row_ref,
    dq_ref, dk_ref, dv_ref, sum_ref, km_ref, vm_ref, kt_ref, dk_acc, dv_acc,
):
    length, lanes = q_ref.shape
    half, heads = 64, lanes // 64
    wide, low = jnp.float32, jnp.bfloat16
    scale = half**-0.5
    for block in range(length // KEYS):
        part = pl.ds(block * KEYS, KEYS)
        km_ref[0, part, :], km_ref[1, part, :] = one_head(k_ref[part, :], half)
        vm_ref[0, part, :], vm_ref[1, part, :] = one_head(v_ref[part, :], half)
        kt_ref[block] = flipped(k_ref[part, :]).astype(low)
    sum_ref[...] = jnp.zeros_like(sum_ref)
    dk_acc[...] = jnp.zeros_like(dk_acc)
    dv_acc[...] = jnp.zeros_like(dv_acc)

    for block in range(length // ROWS):
        rows = pl.ds(block * ROWS, ROWS)
        queries = q_ref[rows, :] * low(scale)
        grads = grad_ref[rows, :]
        row_docs = seg_row_ref[:, rows]
        queries_both = jnp.concatenate(one_head(queries, half), axis=0)
        grads_both = jnp.concatenate(one_head(grads, half), axis=0)
        products = (grads.astype(wide) * mixed_ref[rows, :].astype(wide)).T
        dots = [jnp.sum(products[h * half : (h + 1) * half], axis=0, keepdims=True) for h in range(heads)]
        logs = [log_ref[0, h : h + 1, rows] for h in range(heads)]

        def step(index, carry):
            part = pl.ds(pl.multiple_of(index * KEYS, KEYS), KEYS)
            docs = seg_col_ref[part, :]
            key_docs = jnp.concatenate([docs] * (ROWS // 128), axis=1)
            every = range(heads)
            pairs = [slice(h // 2 * 128, h // 2 * 128 + 128) for h in every]
            scores = [
                head_scores(km_ref[h % 2, part, pairs[h]], queries[:, pairs[h]], key_docs, row_docs) for h in every
            ]
            grad_probs = [
                lax.dot_general(vm_ref[h % 2, part, pairs[h]], grads[:, pairs[h]], NT, preferred_element_type=wide)
                for h in every
            ]
            probs = [jnp.exp(scores[h] - logs[h]) for h in every]
            slopes = [(probs[h] * (grad_probs[h] - dots[h])).astype(low) for h in every]
            keys = [kt_ref[index, h * half : (h + 1) * half, :] for h in every]
            new = [carry[h] + jnp.dot(keys[h], slopes[h], preferred_element_type=wide) for h in every]
            for h in range(0, heads, 2):
                dv_acc[part, pairs[h]] += jnp.dot(
                    jnp.concatenate([probs[h].astype(low), probs[h + 1].astype(low)], axis=1),
                    grads_both[:, pairs[h]],
                    preferred_element_type=wide,
                )
                dk_acc[part, pairs[h]] += jnp.dot(
                    jnp.concatenate(slopes[h : h + 2], axis=1), queries_both[:, pairs[h]], preferred_element_type=wide
                )
            return tuple(new)

        zero = jnp.zeros((half, ROWS), wide)
        dq = lax.fori_loop(lo_ref[block], hi_ref[block], step, (zero,) * heads)
        dq = (jnp.concatenate(dq, axis=0).T * scale).astype(low)
        dq_ref[rows, :] = dq
        sum_ref[0:1, :] += jnp.sum(dq.astype(wide), axis=0, keepdims=True)
    dk_ref[...] = dk_acc[...].astype(low)
    dv = dv_acc[...].astype(low)
    dv_ref[...] = dv
    sum_ref[1:2, :] = jnp.sum(dv.astype(wide), axis=0, keepdims=True)


def key_ranges(doc_ids):
    ends = doc_ids.reshape(-1, ROWS)
    lo = jnp.sum(doc_ids[None, :] < ends[:, :1], axis=1, dtype=jnp.int32) // KEYS
    hi = (jnp.sum(doc_ids[None, :] <= ends[:, -1:], axis=1, dtype=jnp.int32) + KEYS - 1) // KEYS
    return lo, hi


def attend(qkv, docs):
    lo, hi, seg_col, seg_row = docs
    length = qkv.shape[0]
    width = qkv.shape[1] // 3
    lanes = PAIRS * 128
    pairs = width // lanes
    column = lambda base: pl.BlockSpec((length, lanes), lambda i, *_: (0, base * pairs + i))
    whole = lambda shape: pl.BlockSpec(shape, lambda i, *_: (0, 0))
    return pl.pallas_call(
        attend_kernel,
        grid_spec=pltpu.PrefetchScalarGridSpec(
            num_scalar_prefetch=2,
            grid=(pairs,),
            in_specs=[column(0), column(1), column(2), whole((length, 128)), whole((1, length))],
            out_specs=[column(0), pl.BlockSpec((1, 16, length), lambda i, *_: (i, 0, 0))],
            scratch_shapes=[
                pltpu.VMEM((2, length, lanes), jnp.bfloat16),
                pltpu.VMEM((length // KEYS, lanes, KEYS), jnp.bfloat16),
            ],
        ),
        out_shape=[
            jax.ShapeDtypeStruct((length, width), jnp.bfloat16),
            jax.ShapeDtypeStruct((pairs, 16, length), jnp.float32),
        ],
        name="attend",
    )(lo, hi, qkv, qkv, qkv, seg_col, seg_row)


def attend_back(qkv, grad, mixed, logs, docs):
    lo, hi, seg_col, seg_row = docs
    length = qkv.shape[0]
    width = qkv.shape[1] // 3
    lanes = PAIRS * 128
    pairs = width // lanes
    column = lambda base: pl.BlockSpec((length, lanes), lambda i, *_: (0, base * pairs + i))
    whole = lambda shape: pl.BlockSpec(shape, lambda i, *_: (0, 0))
    return pl.pallas_call(
        attend_back_kernel,
        grid_spec=pltpu.PrefetchScalarGridSpec(
            num_scalar_prefetch=2,
            grid=(pairs,),
            in_specs=[column(0), column(1), column(2), column(0), column(0),
                pl.BlockSpec((1, 16, length), lambda i, *_: (i, 0, 0)), whole((length, 128)), whole((1, length))],
            out_specs=[column(0)] * 3 + [pl.BlockSpec((8, lanes), lambda i, *_: (0, i))],
            scratch_shapes=[
                pltpu.VMEM((2, length, lanes), jnp.bfloat16),
                pltpu.VMEM((2, length, lanes), jnp.bfloat16),
                pltpu.VMEM((length // KEYS, lanes, KEYS), jnp.bfloat16),
                pltpu.VMEM((length, lanes), jnp.float32),
                pltpu.VMEM((length, lanes), jnp.float32),
            ],
        ),
        out_shape=[jax.ShapeDtypeStruct((length, width), jnp.bfloat16)] * 3
        + [jax.ShapeDtypeStruct((8, width), jnp.float32)],
        name="attend_back",
    )(lo, hi, qkv, qkv, qkv, grad, mixed, logs, seg_col, seg_row)


def doc_tables(doc_ids):
    lo, hi = key_ranges(doc_ids)
    return lo, hi, jnp.broadcast_to(doc_ids[:, None], (doc_ids.shape[0], 128)), doc_ids[None, :]

def gelu_parts(pre):
    square = 0.5 * pre * pre
    t = 1.0 / (1.0 + (0.5**1.5) * jnp.abs(pre))
    series = 0.17087277
    for term in (-0.82215223, 1.48851587, -1.13520398, 0.27886807, -0.18628806, 0.09678418, 0.37409196, 1.00002368):
        series = term + t * series
    tail = t * jnp.exp(t * series - (1.26551223 + math.log(2.0)) - square)
    below = jnp.where(pre >= 0, 1.0 - tail, tail)
    return pre * below, below + pre * jnp.exp(-square) * ((2.0 * jnp.pi) ** -0.5)


def layer_norm(resid, gain, shift):
    row_mean = jnp.mean(resid, axis=-1, keepdims=True)
    centred = resid - row_mean
    variance = jnp.mean(centred * centred, axis=-1, keepdims=True)
    inv_std = lax.rsqrt(variance + 1e-05)
    normed = centred * inv_std
    return (normed * gain + shift, normed, inv_std)


def norm_back(grad_in, gain, normed, inv_std):
    grad_norm = grad_in * gain
    first = jnp.mean(grad_norm, axis=-1, keepdims=True)
    second = jnp.mean(grad_norm * normed, axis=-1, keepdims=True)
    return inv_std * (grad_norm - first - normed * second)


def project(left, weight, bias):
    return jnp.dot(left, weight, preferred_element_type=jnp.float32) + bias.astype(jnp.float32)


def weight_grad(left, right):
    return jnp.einsum("ti,to->io", left, right, preferred_element_type=jnp.float32)


def back_input(grad_rows, weight):
    return jnp.einsum("to,io->ti", grad_rows, weight, preferred_element_type=jnp.float32)


def col_sum(values):
    return jnp.sum(values.astype(jnp.float32), axis=0)


def owner_blocks(matrices, vectors):
    devices = lax.axis_size("dp")
    width = matrices[0].shape[1]
    pieces, shapes = [], []
    for matrix in matrices:
        low = matrix.astype(jnp.bfloat16)
        own = low.shape[0] // devices
        blocks = low.reshape(devices, own, low.shape[1])
        parts = low.shape[1] // width
        pieces += [blocks[:, :, i * width : (i + 1) * width] for i in range(parts)]
        shapes.append((own, parts))
    if not vectors:
        return jnp.concatenate(pieces, axis=1), (shapes, [])
    flat = [vector.reshape(devices, -1) for vector in vectors]
    lengths = [vector.shape[1] for vector in flat]
    packed = jnp.concatenate(flat, axis=1)
    packed = jnp.pad(packed, ((0, 0), (0, 8 * width - packed.shape[1])))
    pieces.append(packed.reshape(devices, 8, width).astype(jnp.bfloat16))
    return jnp.concatenate(pieces, axis=1), (shapes, lengths)


def own_shares(mine, layout):
    shapes, lengths = layout
    mine = mine.astype(jnp.float32)
    outs, at = [], 0
    for own, parts in shapes:
        outs.append(
            jnp.concatenate([mine[at + i * own : at + (i + 1) * own] for i in range(parts)], axis=1)
        )
        at += own * parts
    tail, at = mine[at:].reshape(-1), 0
    for length in lengths:
        outs.append(tail[at : at + length])
        at += length
    return tuple(outs)


def plane_groups():
    devices = lax.axis_size("dp")
    runs = devices // PLANE
    if devices % PLANE or runs < 2:
        return None
    inner = [[run * PLANE + i for i in range(PLANE)] for run in range(runs)]
    return inner, [[run * PLANE + i for run in range(runs)] for i in range(PLANE)]


def scatter(blocks, stage):
    groups = plane_groups()
    if groups is None:
        return blocks if stage else lax.psum_scatter(blocks, "dp", scatter_dimension=0, tiled=True)
    return lax.psum_scatter(blocks, "dp", scatter_dimension=0, tiled=True, axis_index_groups=groups[stage])


def plane_order(blocks):
    devices = lax.axis_size("dp")
    if devices % PLANE or devices == PLANE:
        return blocks
    parts = blocks.reshape((devices // PLANE, -1) + blocks.shape[1:])
    return parts.swapaxes(0, 1).reshape(blocks.shape)


def double(shards, bit, held):
    devices = lax.axis_size("dp")
    low_count = 2 ** sum(b < bit for b in held)
    view = shards.reshape((shards.shape[0] // low_count, 1, low_count) + shards.shape[1:])
    got = lax.ppermute(view, "dp", [(i, i ^ (1 << bit)) for i in range(devices)])
    upper = ((lax.axis_index("dp") >> bit) & 1) == 1
    both = jnp.concatenate([jnp.where(upper, got, view), jnp.where(upper, view, got)], axis=1)
    return both.reshape((-1,) + shards.shape[1:]), held + [bit]


def doubling_gather(shard, ready):
    devices = lax.axis_size("dp")
    if devices & (devices - 1) or devices < 8:
        return lax.all_gather(shard, "dp", axis=0, tiled=True), ready
    shards, held = shard[None], []
    for bit in range(3, devices.bit_length() - 1):
        shards, held = double(shards, bit, held)
    shards, ready = lax.optimization_barrier((shards, ready))
    middle = shard.shape[1] // 256 * 128
    one, two = shards[:, :, :middle], shards[:, :, middle:]
    one, one_held = double(one, 2, held)
    two, two_held = double(two, 1, held)
    one, one_held = double(one, 1, one_held)
    two, two_held = double(two, 2, two_held)
    one, _ = double(one, 0, one_held)
    two, _ = double(two, 0, two_held)
    both = jnp.concatenate([one, two], axis=2)
    return both.reshape(-1, both.shape[2]), ready


def halve(blocks, bit, left):
    devices = lax.axis_size("dp")
    low_count = 2 ** left.index(bit)
    view = blocks.reshape((blocks.shape[0] // (2 * low_count), 2, low_count) + blocks.shape[1:])
    mine = (lax.axis_index("dp") >> bit) & 1
    kept = lax.dynamic_index_in_dim(view, mine, 1, keepdims=False)
    sent = lax.dynamic_index_in_dim(view, 1 - mine, 1, keepdims=False)
    got = lax.ppermute(sent, "dp", [(i, i ^ (1 << bit)) for i in range(devices)])
    added = (kept.astype(jnp.float32) + got.astype(jnp.float32)).astype(blocks.dtype)
    return added.reshape((-1,) + blocks.shape[1:]), [b for b in left if b != bit]


def halving_sum(blocks):
    devices = lax.axis_size("dp")
    if devices & (devices - 1) or devices < 8:
        return lax.psum_scatter(blocks, "dp", scatter_dimension=0, tiled=True)[0]
    left = list(range(devices.bit_length() - 1))
    blocks, left = halve(blocks, 0, left)
    middle = blocks.shape[1] // 16 * 8
    one, two = blocks[:, :middle], blocks[:, middle:]
    one, one_left = halve(one, 1, left)
    two, two_left = halve(two, 2, left)
    one, one_left = halve(one, 2, one_left)
    two, two_left = halve(two, 1, two_left)
    blocks, left = jnp.concatenate([one, two], axis=1), one_left
    for bit in list(left):
        blocks, left = halve(blocks, bit, left)
    return blocks[0]


def shards(
    layer_input,
    segments,
    cotangent,
    w_query,
    b_query,
    w_key,
    w_value,
    b_value,
    w_out,
    b_out,
    norm1_gain,
    norm1_bias,
    w_in,
    b_in,
    w_down,
    b_down,
    norm2_gain,
    norm2_bias,
):
    low_type = jnp.bfloat16
    wide_type = jnp.float32
    own_rows, width = w_query.shape
    hidden = w_in.shape[1]
    fold = hidden // width
    vectors = (b_query, b_value, b_out, norm1_gain, norm1_bias, b_down, norm2_gain, norm2_bias)
    places = jnp.eye(len(vectors), 128, dtype=low_type)
    columns = jnp.einsum("vr,vc->rc", jnp.stack(vectors), places, preferred_element_type=wide_type).astype(low_type)
    columns = lax.dynamic_update_slice(columns, b_in.reshape(own_rows, fold), (0, len(vectors)))
    first, (tokens_over, cotangent_over) = doubling_gather(
        jnp.concatenate([w_query, w_key, w_value, columns], axis=1), (layer_input[0].T, cotangent[0].T)
    )
    full_qkv, full_columns = first[:, : 3 * width], first[:, 3 * width :]
    in_parts = [w_in[:, i * width : (i + 1) * width] for i in range(fold)]
    packed = jnp.concatenate([w_out] + in_parts + [w_down], axis=0)
    gathered = lax.all_gather(packed[None], "dp", axis=0, tiled=True)
    pieces = [gathered[:, i * own_rows : (i + 1) * own_rows].reshape(width, width) for i in range(1 + fold)]
    full_wo, full_win = pieces[0], jnp.concatenate(pieces[1:], axis=1)
    full_wdown = gathered[:, (1 + fold) * own_rows :].reshape(hidden, width)
    vector_rows = full_columns.T.astype(wide_type)
    full_bq, full_bv, full_bo, gain_one, shift_one, full_bdown, gain_two, shift_two = (
        vector_rows[i] for i in range(8)
    )
    full_bin = full_columns[:, 8 : 8 + fold].astype(wide_type).reshape(-1)

    tokens = layer_input[0]
    docs = doc_tables(segments[0])
    bias = jnp.concatenate([full_bq, jnp.zeros_like(full_bq), full_bv])
    qkv = project(tokens, full_qkv, bias).astype(low_type)
    context, log_total = attend(qkv, docs)
    resid_one = tokens_over.T.astype(wide_type) + project(context, full_wo, full_bo)
    hidden_one, normed_one, inv_one = layer_norm(resid_one, gain_one, shift_one)
    hidden_low = lax.optimization_barrier(hidden_one.astype(low_type))
    activated, slope = gelu_parts(project(hidden_low, full_win, full_bin))
    act_low, slope = lax.optimization_barrier((activated.astype(low_type), slope.astype(low_type)))
    resid_two = hidden_one + project(act_low, full_wdown, full_bdown)
    outputs, normed_two, inv_two = layer_norm(resid_two, gain_two, shift_two)
    layer_out = outputs.astype(low_type)[None]

    grad_out = cotangent_over.T.astype(wide_type)
    grad_gain_two = jnp.sum(grad_out * normed_two, axis=0)
    grad_shift_two = jnp.sum(grad_out, axis=0)
    grad_resid_two = norm_back(grad_out, gain_two, normed_two, inv_two)
    grad_ffn = grad_resid_two.astype(low_type)
    grad_bdown = col_sum(grad_ffn)
    down_blocks = owner_blocks((weight_grad(act_low, grad_ffn),), ())[0]
    down_blocks, grad_ffn = lax.optimization_barrier((plane_order(down_blocks), grad_ffn))
    down_part = scatter(down_blocks, 0)
    grad_pre = (back_input(grad_ffn, full_wdown) * slope.astype(wide_type)).astype(low_type)
    grad_bin = col_sum(grad_pre)
    grad_win = weight_grad(hidden_low, grad_pre)
    grad_hidden = grad_resid_two + back_input(grad_pre, full_win)
    grad_gain_one = jnp.sum(grad_hidden * normed_one, axis=0)
    grad_shift_one = jnp.sum(grad_hidden, axis=0)
    grad_resid_one = norm_back(grad_hidden, gain_one, normed_one, inv_one)
    grad_attn = grad_resid_one.astype(low_type)
    grad_bo = col_sum(grad_attn)
    grad_wo = weight_grad(context, grad_attn)
    ffn_blocks, ffn_layout = owner_blocks((grad_wo, grad_win), ())
    ffn_blocks = plane_order(ffn_blocks)
    grad_context = back_input(grad_attn, full_wo).astype(low_type)
    ffn_blocks, grad_context = lax.optimization_barrier((ffn_blocks, grad_context))
    ffn_part = scatter(ffn_blocks, 0)
    ffn_mine = scatter(jnp.concatenate([down_part, ffn_part], axis=1), 1)[0]
    own_down_rows = w_down.shape[0]

    grad_query, grad_key, grad_value, sums = attend_back(qkv, grad_context, context, log_total, docs)
    attn_blocks, attn_layout = owner_blocks(
        tuple(weight_grad(tokens, grad) for grad in (grad_query, grad_key, grad_value)),
        (
            sums[0],
            sums[1],
            grad_bo,
            grad_gain_one,
            grad_shift_one,
            grad_bin,
            grad_bdown,
            grad_gain_two,
            grad_shift_two,
        ),
    )
    attn_mine = halving_sum(attn_blocks)
    grad_tokens = (
        grad_resid_one
        + back_input(grad_query, full_qkv[:, :width])
        + back_input(grad_key, full_qkv[:, width : 2 * width])
        + back_input(grad_value, full_qkv[:, 2 * width :])
    )
    (
        own_wq,
        own_wk,
        own_wv,
        own_bq,
        own_bv,
        own_bo,
        own_gain_one,
        own_shift_one,
        own_bin,
        own_bdown,
        own_gain_two,
        own_shift_two,
    ) = own_shares(attn_mine, attn_layout)
    own_wo, own_win = own_shares(ffn_mine[own_down_rows:], ffn_layout)
    own_wdown = ffn_mine[:own_down_rows].astype(wide_type)
    return (
        layer_out,
        grad_tokens[None],
        own_wq,
        own_bq,
        own_wk,
        own_wv,
        own_bv,
        own_wo,
        own_bo,
        own_gain_one,
        own_shift_one,
        own_win,
        own_bin,
        own_wdown,
        own_bdown,
        own_gain_two,
        own_shift_two,
    )


def solution(mesh):
    placed = (
        P("dp", None, None),
        P("dp", None),
        P("dp", None, None),
        P("dp", None),
        P("dp"),
        P("dp", None),
        P("dp", None),
        P("dp"),
        P("dp", None),
        P("dp"),
        P("dp"),
        P("dp"),
        P("dp", None),
        P("dp"),
        P("dp", None),
        P("dp"),
        P("dp"),
        P("dp"),
    )
    return jax.shard_map(
        shards,
        mesh=mesh,
        in_specs=placed,
        out_specs=(
            P("dp", None, None),
            P("dp", None, None),
            P("dp", None),
            P("dp"),
            P("dp", None),
            P("dp", None),
            P("dp"),
            P("dp", None),
            P("dp"),
            P("dp"),
            P("dp"),
            P("dp", None),
            P("dp"),
            P("dp", None),
            P("dp"),
            P("dp"),
            P("dp"),
        ),
        check_vma=False,
    )
```
